32 devices in a mesh: rep: 8 (over z, x), grp: 4 (over y, core).
Axes of the slice: x: 2, y: 2, z: 4, core: 2. Of those that a mesh axis runs over, the one named last changes fastest.
Arguments:
- images: bfloat16 [128, 197, 384], P(('rep', 'grp')), may hold values from -6 to 6
- cotangent: bfloat16 [128, 197, 384], P(('rep', 'grp')), may hold values from -6 to 6
- counts: int32 [32], P(('rep', 'grp')), may hold values from 1 to 4, as said below
- ln1_gain: bfloat16 [384], P('grp'), may hold values from 0.25 to 1.75
- ln1_bias: bfloat16 [384], P('grp'), may hold values from -3 to 3
- w_qkv: bfloat16 [384, 1152], P('grp'), may hold values from -0.3125 to 0.3125
- b_query: bfloat16 [384], P('grp'), may hold values from -4 to 4
- b_value: bfloat16 [384], P('grp'), may hold values from -2 to 2
- w_out: bfloat16 [384, 384], P('grp'), may hold values from -1.25 to 1.25
- b_out: bfloat16 [384], P('grp'), may hold values from -3 to 3
- ln2_gain: bfloat16 [384], P('grp'), may hold values from 0.25 to 1.75
- ln2_bias: bfloat16 [384], P('grp'), may hold values from -3 to 3
- w_fc1: bfloat16 [384, 1536], P('grp'), may hold values from -0.3125 to 0.3125
- b_fc1: bfloat16 [1536], P('grp'), may hold values from -3 to 3
- w_fc2: bfloat16 [1536, 384], P('grp'), may hold values from -0.15625 to 0.15625
- b_fc2: bfloat16 [384], P('grp'), may hold values from -3 to 3
Outputs:
- block_out: bfloat16 [128, 197, 384], P(('rep', 'grp'))
- images_grad: float32 [128, 197, 384], P(('rep', 'grp'))
- ln1_gain_grad: float32 [384], P('grp')
- ln1_bias_grad: float32 [384], P('grp')
- w_qkv_grad: float32 [384, 1152], P('grp')
- b_query_grad: float32 [384], P('grp')
- b_value_grad: float32 [384], P('grp')
- w_out_grad: float32 [384, 384], P('grp')
- b_out_grad: float32 [384], P('grp')
- ln2_gain_grad: float32 [384], P('grp')
- ln2_bias_grad: float32 [384], P('grp')
- w_fc1_grad: float32 [384, 1536], P('grp')
- b_fc1_grad: float32 [1536], P('grp')
- w_fc2_grad: float32 [1536, 384], P('grp')
- b_fc2_grad: float32 [384], P('grp')
The draws below stay inside these ranges and needn't reach their ends.
Inputs may be any that keep to these rules, and one draw needn't show every extreme that they name: counts[i] is the number of live image slots of device i (devices in the order rep, then grp); some device holds 4 live images and some exactly one.
All inputs are finite; a program needn't handle non-finite values.
Results may differ from the reference program's by a relative error of at most 0.02.
Values may be sent and summed in bfloat16 or wider, within the bound.
No kernel may reach another device: no remote copies, remote signals or barrier semaphores. Data moves between devices by JAX's collectives and lax.ppermute only.
A program may use at most 128 MiB of HBM per device.

```python
import jax
import jax.numpy as jnp
from jax import lax

D = 384
HEAD_DIM = 64
FF = 1536
S = 197
IMG_CAP = 4
IMAGES = 128
DEVICES = 32


def draw_counts(key, part):
    first, second, third = jax.random.split(jax.random.fold_in(key, 7), 3)
    counts = jax.random.randint(first, (DEVICES,), 1, IMG_CAP + 1)
    top = jax.random.randint(second, (), 0, DEVICES)
    low = (top + jax.random.randint(third, (), 1, DEVICES)) % DEVICES
    places = jnp.arange(DEVICES)
    counts = jnp.where(places == top, IMG_CAP, counts)
    counts = jnp.where(places == low, 1, counts)
    return counts.astype(jnp.int32)


def steps_of(own_key, shape, pieces, low, largest):
    loudness = 1.0
    for dim, shards_of in pieces:
        draws = jax.random.uniform(jax.random.fold_in(jax.random.fold_in(own_key, 6), dim), (shards_of,), jnp.float32, low / len(pieces), largest / len(pieces))
        loudness = loudness * jnp.repeat(jnp.exp(draws), shape[dim] // shards_of).reshape((-1,) + (1,) * (len(shape) - 1 - dim))
    return loudness


def noise(stream_key, extent, scale, bound, cuts=(), kind=jnp.bfloat16):
    result = scale * jax.random.normal(stream_key, extent, jnp.float32)
    if cuts:
        result = result * steps_of(stream_key, extent, cuts, -0.22, 0.18)
    return jnp.clip(result, -bound, bound).astype(kind)


def setup_inputs(seed: int = 0) -> dict:
    key_list = jax.random.split(jax.random.key(seed), 17)
    return {
        "images": noise(key_list[0], (IMAGES, S, D), 1.0, 6.0, ((0, 32),)),
        "cotangent": noise(key_list[1], (IMAGES, S, D), 1.0, 6.0, ((0, 32),)),
        "counts": draw_counts(jax.random.fold_in(key_list[16], 71), 0),
        "ln1_gain": jnp.clip(1.0 + 0.15 * jax.random.normal(key_list[3], (D,), jnp.float32), 0.25, 1.75).astype(jnp.bfloat16),
        "ln1_bias": noise(key_list[4], (D,), 0.5, 3.0, ((0, 4),)),
        "w_qkv": noise(key_list[5], (D, 3 * D), D ** -0.5, 0.3125, ((0, 4),)),
        "b_query": noise(key_list[6], (D,), 1.0, 4.0, ((0, 4),)),
        "b_value": noise(key_list[7], (D,), 0.3, 2.0, ((0, 4),)),
        "w_out": noise(key_list[8], (D, D), (D // 16) ** -0.5, 1.25, ((0, 4),)),
        "b_out": noise(key_list[9], (D,), 0.5, 3.0, ((0, 4),)),
        "ln2_gain": jnp.clip(1.0 + 0.15 * jax.random.normal(key_list[10], (D,), jnp.float32), 0.25, 1.75).astype(jnp.bfloat16),
        "ln2_bias": noise(key_list[11], (D,), 0.5, 3.0, ((0, 4),)),
        "w_fc1": noise(key_list[12], (D, FF), D ** -0.5, 0.3125, ((0, 4),)),
        "b_fc1": noise(key_list[13], (FF,), 0.5, 3.0, ((0, 4),)),
        "w_fc2": noise(key_list[14], (FF, D), FF ** -0.5, 0.15625, ((0, 4),)),
        "b_fc2": noise(key_list[15], (D,), 0.5, 3.0, ((0, 4),)),
    }


EPS = 1e-06
INV_ROOT2 = 0.7071067811865476
INV_ROOT2PI = 0.3989422804014327

def prod(form, left, right):
    return jnp.einsum(form, left.astype(jnp.float32), right.astype(jnp.float32))

def flatten(a):
    return a.reshape(-1, a.shape[-1])

def dense(a, weight):
    out = jnp.dot(flatten(a), weight, preferred_element_type=jnp.float32)
    return out.reshape(a.shape[:-1] + (weight.shape[1],))

def dense_back(a, weight):
    out = lax.dot_general(flatten(a), weight, (((1,), (1,)), ((), ())), preferred_element_type=jnp.float32)
    return out.reshape(a.shape[:-1] + (weight.shape[0],))

def outer_sum(left, right):
    return lax.dot_general(flatten(left), flatten(right), (((0,), (0,)), ((), ())), preferred_element_type=jnp.float32)

def summed_rows(a):
    return lax.optimization_barrier(jnp.sum(flatten(a), 0))

def apply_layer_norm(value, norm_gain, norm_bias):
    row_average = lax.optimization_barrier(jnp.mean(value, -1, keepdims=True))
    centred_rows = value - row_average
    reciprocal_deviation = lax.rsqrt(lax.optimization_barrier(jnp.mean(centred_rows * centred_rows, -1, keepdims=True)) + EPS)
    standardized_input = centred_rows * reciprocal_deviation
    return (standardized_input, reciprocal_deviation, standardized_input * norm_gain.astype(jnp.float32) + norm_bias.astype(jnp.float32))

def layer_norm_backward(upstream_gradient, standardized_input, reciprocal_deviation, norm_gain):
    scaled_rows = upstream_gradient * norm_gain.astype(jnp.float32)
    inner_product = scaled_rows - lax.optimization_barrier(jnp.mean(scaled_rows, -1, keepdims=True)) - standardized_input * lax.optimization_barrier(jnp.mean(scaled_rows * standardized_input, -1, keepdims=True))
    return (reciprocal_deviation * inner_product, summed_rows(upstream_gradient * standardized_input), summed_rows(upstream_gradient))

def gelu_value(u):
    return 0.5 * u * (1.0 + jax.scipy.special.erf(u * INV_ROOT2))

def gelu_slope(u):
    return 0.5 * (1.0 + jax.scipy.special.erf(u * INV_ROOT2)) + u * jnp.exp(-0.5 * u * u) * INV_ROOT2PI

def encoder_forward(images, layer_parameters):
    first_norm_gain, first_centred_rows, w_qkv, b_query, b_value, w_out, b_out, second_norm_gain, second_centred_rows, w_fc1, b_fc1, w_fc2, b_fc2 = layer_parameters
    width = images.shape[-1]
    split = images.shape[:-1] + (width // HEAD_DIM, HEAD_DIM)
    scale = HEAD_DIM ** (-0.5)
    gathered_input = images.astype(jnp.float32)
    standardized_input1, reciprocal_deviation1, normed_rows = apply_layer_norm(gathered_input, first_norm_gain, first_centred_rows)
    first_residual_sum = normed_rows.astype(jnp.bfloat16)
    qkv = dense(first_residual_sum, w_qkv)
    query_rows = (qkv[..., :width] + b_query.astype(jnp.float32)).astype(jnp.bfloat16).reshape(split)
    key_rows = qkv[..., width:2 * width].astype(jnp.bfloat16).reshape(split)
    value_rows = (qkv[..., 2 * width:] + b_value.astype(jnp.float32)).astype(jnp.bfloat16).reshape(split)
    scores = prod('bqhd,bkhd->bhqk', query_rows, key_rows) * scale
    logsumexp_scores = jnp.log(lax.optimization_barrier(jnp.sum(jnp.exp(scores), -1, keepdims=True)))
    probs = jnp.exp(scores - logsumexp_scores).astype(jnp.bfloat16)
    attention_result = prod('bhqk,bkhd->bqhd', probs, value_rows).astype(jnp.bfloat16)
    residual_stream = gathered_input + dense(attention_result.reshape(images.shape), w_out) + b_out.astype(jnp.float32)
    standardized_input2, reciprocal_deviation2, second_normed_rows = apply_layer_norm(residual_stream, second_norm_gain, second_centred_rows)
    second_residual_sum = second_normed_rows.astype(jnp.bfloat16)
    hidden_units = dense(second_residual_sum, w_fc1) + b_fc1.astype(jnp.float32)
    activated_hidden = gelu_value(hidden_units).astype(jnp.bfloat16)
    layer_result = residual_stream + dense(activated_hidden, w_fc2) + b_fc2.astype(jnp.float32)
    return (first_residual_sum, query_rows, key_rows, value_rows, logsumexp_scores, attention_result, standardized_input1, reciprocal_deviation1, standardized_input2, reciprocal_deviation2, second_residual_sum, hidden_units, activated_hidden, layer_result)

def backward(images, cotangent, live, layer_parameters):
    first_norm_gain, first_centred_rows, w_qkv, b_query, b_value, w_out, b_out, second_norm_gain, second_centred_rows, w_fc1, b_fc1, w_fc2, b_fc2 = layer_parameters
    first_residual_sum, query_rows, key_rows, value_rows, logsumexp_scores, attention_result, standardized_input1, reciprocal_deviation1, standardized_input2, reciprocal_deviation2, second_residual_sum, hidden_units, activated_hidden, layer_result = encoder_forward(images, layer_parameters)
    scale = HEAD_DIM ** (-0.5)
    grad_y = cotangent.astype(jnp.float32) * live
    grad_yb = grad_y.astype(jnp.bfloat16)
    grad_w2 = outer_sum(activated_hidden, grad_yb)
    grad_b2 = summed_rows(grad_y)
    grad_u = dense_back(grad_yb, w_fc2) * gelu_slope(hidden_units)
    grad_b1 = summed_rows(grad_u)
    grad_ub = grad_u.astype(jnp.bfloat16)
    grad_w1 = outer_sum(second_residual_sum, grad_ub)
    second_residual_gradient = dense_back(grad_ub, w_fc1)
    second_normed_gradient, second_gain_gradient, second_centred_gradient = layer_norm_backward(second_residual_gradient, standardized_input2, reciprocal_deviation2, second_norm_gain)
    grad_h = grad_y + second_normed_gradient
    grad_hb = grad_h.astype(jnp.bfloat16)
    grad_wo = outer_sum(attention_result.reshape(images.shape), grad_hb)
    grad_bo = summed_rows(grad_h)
    grad_o = dense_back(grad_hb, w_out).astype(jnp.bfloat16).reshape(query_rows.shape)
    grad_p = prod('bqhd,bkhd->bhqk', grad_o, value_rows)
    probs_full = jnp.exp(prod('bqhd,bkhd->bhqk', query_rows, key_rows) * scale - logsumexp_scores)
    probs = probs_full.astype(jnp.bfloat16)
    grad_v = prod('bhqk,bqhd->bkhd', probs, grad_o)
    delta = lax.optimization_barrier(jnp.sum(grad_o.astype(jnp.float32) * attention_result.astype(jnp.float32), -1))
    delta = jnp.moveaxis(delta, 2, 1)[..., None]
    grad_s = (probs_full * (grad_p - delta)).astype(jnp.bfloat16)
    grad_q = prod('bhqk,bkhd->bqhd', grad_s, key_rows) * scale
    grad_k = prod('bhqk,bqhd->bkhd', grad_s, query_rows) * scale
    flat = images.shape
    grad_qkv = jnp.concatenate([grad_q.reshape(flat), grad_k.reshape(flat), grad_v.reshape(flat)], -1)
    grad_bq = summed_rows(grad_q.reshape(flat))
    grad_bv = summed_rows(grad_v.reshape(flat))
    grad_qkvb = grad_qkv.astype(jnp.bfloat16)
    grad_wqkv = outer_sum(first_residual_sum, grad_qkvb)
    first_residual_gradient = dense_back(grad_qkvb, w_qkv)
    first_normed_gradient, first_gain_gradient, first_centred_gradient = layer_norm_backward(first_residual_gradient, standardized_input1, reciprocal_deviation1, first_norm_gain)
    grad_x = grad_h + first_normed_gradient
    output = (layer_result * live).astype(jnp.bfloat16)
    grads = (first_gain_gradient, first_centred_gradient, grad_wqkv, grad_bq, grad_bv, grad_wo, grad_bo, second_gain_gradient, second_centred_gradient, grad_w1, grad_b1, grad_w2, grad_b2)
    return (output, grad_x, grads)

def reference(images, cotangent, counts, ln1_gain, ln1_bias, w_qkv, b_query, b_value, w_out, b_out, ln2_gain, ln2_bias, w_fc1, b_fc1, w_fc2, b_fc2):
    layer_parameters = (ln1_gain, ln1_bias, w_qkv, b_query, b_value, w_out, b_out, ln2_gain, ln2_bias, w_fc1, b_fc1, w_fc2, b_fc2)
    slots = images.shape[0]
    index = jnp.arange(slots).astype(jnp.int32)
    live_all = (index % IMG_CAP < counts[index // IMG_CAP]).astype(jnp.float32)
    zero_grads = tuple((jnp.zeros(p.shape, jnp.float32) for p in layer_parameters))

    def step(carry, item):
        image, grad_out, alive = item

        def run(unused):
            output, grad_x, grads = backward(image[None], grad_out[None], alive.reshape(1, 1, 1), layer_parameters)
            return (output[0], grad_x[0], grads)

        def skip(unused):
            return (jnp.zeros(image.shape, jnp.bfloat16), jnp.zeros(image.shape, jnp.float32), zero_grads)
        output, grad_x, grads = lax.cond(alive > 0.5, run, skip, 0)
        carry = tuple((c + g for c, g in zip(carry, grads)))
        return (carry, (output, grad_x))
    totals, stacked = lax.scan(step, zero_grads, (images, cotangent, live_all))
    outputs, grad_images = stacked
    return (outputs, grad_images, totals[0], totals[1], totals[2], totals[3], totals[4], totals[5], totals[6], totals[7], totals[8], totals[9], totals[10], totals[11], totals[12])
```

```python
import functools
import jax
import jax.numpy as jnp
from jax import lax
from jax.experimental import pallas as pl
from jax.experimental.pallas import tpu as pltpu
from jax.sharding import PartitionSpec as P

HEAD_DIM = 64
EPS = 1e-06
INV_ROOT2 = 0.7071067811865476
INV_ROOT2PI = 0.3989422804014327
F32 = jnp.float32
BF = jnp.bfloat16
VROWS = 16


def nn(a, b):
    return lax.dot_general(a, b, (((1,), (0,)), ((), ())), preferred_element_type=F32)


def nt(a, b):
    return lax.dot_general(a, b, (((1,), (1,)), ((), ())), preferred_element_type=F32)


def norm_stats(r):
    mean = jnp.mean(r, -1, keepdims=True)
    c = r - mean
    rstd = lax.rsqrt(jnp.mean(c * c, -1, keepdims=True) + EPS)
    return c * rstd, rstd


def norm_back(g_out, xhat, rstd, gain):
    g = g_out * gain
    return rstd * (g - jnp.mean(g, -1, keepdims=True) - xhat * jnp.mean(g * xhat, -1, keepdims=True))


def erf_poly(x_abs, e):
    t = 1.0 / (1.0 + 0.3275911 * x_abs)
    return t * (0.254829592 + t * (-0.284496736 + t * (1.421413741 + t * (-1.453152027 + t * 1.061405429)))) * e


def gelu_both(u):
    e = jnp.exp(-0.5 * u * u)
    half_tail = 0.5 * erf_poly(jnp.abs(u) * INV_ROOT2, e)
    cdf = jnp.where(u > 0, 1.0 - half_tail, half_tail)
    return u * cdf, cdf + u * e * INV_ROOT2PI


def load_rows(pieces, dst, sem, g, rows, start=0, col=None):
    copies = []
    for m, p in enumerate(pieces):
        off = pl.multiple_of((g ^ m) * rows, rows & -rows)
        to = dst.at[pl.ds(off, rows), :] if col is None else dst.at[pl.ds(off, rows), pl.ds(col, p.shape[-1])]
        copies.append(pltpu.make_async_copy(p.at[pl.ds(start, rows), :], to, sem.at[m]))
    return copies


def load_rest(pieces, wo_s, w1_s, w2_s, sem, g, rows, frows):
    d = wo_s.shape[1]
    c2 = load_rows(pieces, w2_s, sem.at[0], g, frows)
    c1 = []
    for b in range(w1_s.shape[1] // d):
        c1 += load_rows(pieces, w1_s, sem.at[2 + b], g, rows, frows + b * rows, b * d)
    co = load_rows(pieces, wo_s, sem.at[1], g, rows, 2 * frows)
    return co, c1, c2


def attn_fwd_kernel(n_g, s_len, *refs):
    g_ref, x_ref = refs[:2]
    pieces = refs[2 : 2 + n_g]
    (q_o, k_o, v_o, o_o, kt_o, ot_o, at_o, p_o, vec_o, bf1_o) = refs[2 + n_g : 12 + n_g]
    w_s, xs, vp_s, sem, vsem = refs[12 + n_g :]
    i = pl.program_id(0)
    d = x_ref.shape[-1]
    rows = d // n_g
    t = xs.shape[0]
    g = g_ref[0]

    @pl.when(i == 0)
    def _():
        cps = load_rows(pieces, w_s, sem, g, rows)
        vps = [
            pltpu.make_async_copy(p.at[pl.ds(rows, VROWS), :], vp_s.at[m], vsem.at[m])
            for m, p in enumerate(pieces)
        ]
        for c in cps + vps:
            c.start()
        xs[...] = jnp.zeros_like(xs)
        for c in cps + vps:
            c.wait()
        acc = jnp.zeros((VROWS, d), F32)
        ff = bf1_o.shape[1]
        accf = jnp.zeros((8, ff), F32)
        for m in range(n_g):
            v = vp_s[m].astype(F32)
            acc = acc + pltpu.roll(v[:, :d], (g ^ m) * rows, 1)
            b = v[8:16, :]
            b = jnp.concatenate([b, jnp.zeros((8, ff - b.shape[1]), F32)], 1)
            accf = accf + pltpu.roll(b, (g ^ m) * (ff // n_g), 1)
        vec_o[...] = acc
        bf1_o[...] = accf

    xs[0:s_len, :] = x_ref[0].astype(F32)
    xhat, _ = norm_stats(xs[...])
    a1 = xhat * vec_o[0:1, :] + vec_o[1:2, :]
    at_o[0] = a1.T.astype(BF)
    qkv = nn(a1.astype(BF), w_s[...])
    q = ((qkv[:, :d] + vec_o[2:3, :]) * (HEAD_DIM**-0.5)).astype(BF)
    kf = qkv[:, d : 2 * d]
    k = kf.astype(BF)
    vf = qkv[:, 2 * d :] + vec_o[3:4, :]
    q_o[0] = q
    k_o[0] = k
    v_o[0] = vf.astype(BF)
    kt_o[0] = kf.T.astype(BF)
    vt = vf.T.astype(BF)
    lane = lax.broadcasted_iota(jnp.int32, (t, 2 * HEAD_DIM), 1)
    key = lax.broadcasted_iota(jnp.int32, (t, t), 0)
    for p in range(d // (2 * HEAD_DIM)):
        c = 2 * HEAD_DIM * p
        kp = k[:, c : c + 2 * HEAD_DIM]
        qp = q[:, c : c + 2 * HEAD_DIM]
        parts = []
        for h in range(2):
            keep = (lane < HEAD_DIM) if h == 0 else (lane >= HEAD_DIM)
            st = nt(jnp.where(keep, kp, jnp.zeros_like(kp)), qp)
            e = jnp.where(key < s_len, jnp.exp(st), 0.0)
            pt = (e * (1.0 / jnp.sum(e, 0, keepdims=True))).astype(BF)
            p_o[0, 2 * p + h] = pt
            r0 = c + h * HEAD_DIM
            parts.append(nn(vt[r0 : r0 + HEAD_DIM, :], pt))
        otp = jnp.concatenate(parts, 0)
        ot_o[0, c : c + 2 * HEAD_DIM, :] = otp.astype(BF)
        o_o[0, :, c : c + 2 * HEAD_DIM] = otp.T.astype(BF)


def attn_fwd(g, images, pieces, n_g, ff):
    n, s_len, d = images.shape
    t = -(-s_len // 16) * 16
    heads = d // HEAD_DIM
    rows = d // n_g
    nat = jax.ShapeDtypeStruct((n, t, d), BF)
    tra = jax.ShapeDtypeStruct((n, d, t), BF)
    img = pl.BlockSpec((1, t, d), lambda i: (i, 0, 0))
    imt = pl.BlockSpec((1, d, t), lambda i: (i, 0, 0))
    return pl.pallas_call(
        functools.partial(attn_fwd_kernel, n_g, s_len),
        grid=(n,),
        in_specs=[
            pl.BlockSpec(memory_space=pltpu.SMEM),
            pl.BlockSpec((1, s_len, d), lambda i: (i, 0, 0)),
        ]
        + [pl.BlockSpec(memory_space=pl.ANY)] * n_g,
        out_specs=[img, img, img, img, imt, imt, imt]
        + [
            pl.BlockSpec((1, heads, t, t), lambda i: (i, 0, 0, 0)),
            pl.BlockSpec((VROWS, d), lambda i: (0, 0)),
            pl.BlockSpec((8, ff), lambda i: (0, 0)),
        ],
        out_shape=[nat, nat, nat, nat, tra, tra, tra]
        + [
            jax.ShapeDtypeStruct((n, heads, t, t), BF),
            jax.ShapeDtypeStruct((VROWS, d), F32),
            jax.ShapeDtypeStruct((8, ff), F32),
        ],
        scratch_shapes=[
            pltpu.VMEM((d, 3 * d), BF),
            pltpu.VMEM((t, d), F32),
            pltpu.VMEM((n_g, VROWS, 3 * d), BF),
            pltpu.SemaphoreType.DMA((n_g,)),
            pltpu.SemaphoreType.DMA((n_g,)),
        ],
        name="attn_fwd",
        compiler_params=pltpu.CompilerParams(vmem_limit_bytes=60 * 2**20),
    )(g, images, *pieces)


def mlp_kernel(n_g, s_len, *refs):
    g_ref, cnt_ref, x_ref, o_ref, cot_ref, vec_ref, bf1_ref = refs[:7]
    refs = refs[7:]
    rest = refs[:n_g]
    h_o, z_o, gu_o, keep_o, send_o, gb_o = refs[n_g : n_g + 6]
    wo_s, w1_s, w2_s, xs, gy_s, gyt_s, a2_s, a2t_s, g1_s, g2_s, sem, osem = refs[n_g + 6 :]
    c = pl.program_id(0)
    n, _, d = x_ref.shape
    t = xs.shape[0]
    ff = w1_s.shape[1]
    nc = ff // d
    rows = d // n_g
    frows = ff // n_g
    g = g_ref[0]

    @pl.when(c == 0)
    def _():
        co, c1, c2 = load_rest(rest, wo_s, w1_s, w2_s, sem, g, rows, frows)
        for cp in co + c1 + c2:
            cp.start()
        xs[...] = jnp.zeros_like(xs)
        gb_o[...] = jnp.zeros_like(gb_o)
        for i in range(n):
            live = (i < cnt_ref[0]).astype(F32)
            xs[0:s_len, :] = cot_ref[i].astype(F32) * live
            gy = xs[...]
            gy_s[i] = gy.astype(BF)
            gyt_s[i] = gy.T.astype(BF)
            gb_o[0:1, 0:d] += jnp.sum(gy, 0, keepdims=True)
        for cp in co:
            cp.wait()
        for i in range(n):
            xs[0:s_len, :] = x_ref[i].astype(F32)
            h = xs[...] + nn(o_ref[i], wo_s[...]) + vec_ref[4:5, :]
            h_o[i] = h
            xhat, _ = norm_stats(h)
            a2 = xhat * vec_ref[5:6, :] + vec_ref[6:7, :]
            a2_s[i] = a2.astype(BF)
            a2t_s[i] = a2.T.astype(BF)
        for cp in c1 + c2:
            cp.wait()

    off = pl.multiple_of(c * d, 128)
    w1c = w1_s[:, pl.ds(off, d)]
    w2c = w2_s[pl.ds(off, d), :]
    b1c = bf1_ref[0:1, pl.ds(off, d)]
    g1 = jnp.zeros((d, d), F32)
    g2 = jnp.zeros((d, d), F32)
    gb = jnp.zeros((1, d), F32)
    for i in range(n):
        u = nn(a2_s[i], w1c) + b1c
        gz = nt(gy_s[i], w2c)
        z, slope = gelu_both(u)
        gu = gz * slope
        gb = gb + jnp.sum(gu, 0, keepdims=True)
        zb = z.astype(BF)
        gub = gu.astype(BF)
        z_o[i] = zb
        gu_o[i] = gub
        g2 = g2 + nn(gyt_s[i], zb)
        g1 = g1 + nn(a2t_s[i], gub)
    gb_o[1:2, pl.ds(off, d)] = gb
    g1_s[c] = g1.astype(BF)
    g2_s[pl.ds(off, d), :] = g2.T.astype(BF)

    @pl.when(c == nc - 1)
    def _():
        low = g & 1
        for parity in range(2):
            @pl.when(low == parity)
            def _():
                cps = []
                for s in range(n_g):
                    dst = keep_o if (s & 1) == parity else send_o
                    j = s // 2
                    k = len(cps)
                    cps.append(pltpu.make_async_copy(g2_s.at[pl.ds(s * frows, frows), :], dst.at[j, pl.ds(0, frows), :], osem.at[k]))
                    for b in range(nc):
                        k = len(cps)
                        cps.append(pltpu.make_async_copy(g1_s.at[b, pl.ds(s * rows, rows), :], dst.at[j, pl.ds(frows + b * rows, rows), :], osem.at[k]))
                for cp in cps:
                    cp.start()
                for cp in cps:
                    cp.wait()


def mlp(g, counts, images, o, cot, vec, bf1, rest, n_g):
    n, s_len, d = images.shape
    t = o.shape[1]
    ff = bf1.shape[1]
    nc = ff // d
    srows = ff // n_g + nc * (d // n_g)
    full = lambda shape: pl.BlockSpec(shape, lambda c: (0,) * len(shape))
    anyspec = pl.BlockSpec(memory_space=pl.ANY)
    smem = pl.BlockSpec(memory_space=pltpu.SMEM)
    half = jax.ShapeDtypeStruct((n_g // 2, srows, d), BF)
    return pl.pallas_call(
        functools.partial(mlp_kernel, n_g, s_len),
        grid=(nc,),
        in_specs=[smem, smem, full(images.shape), full(o.shape), full(cot.shape), full(vec.shape), full(bf1.shape)]
        + [anyspec] * n_g,
        out_specs=[
            full((n, t, d)),
            pl.BlockSpec((n, t, d), lambda c: (0, 0, c)),
            pl.BlockSpec((n, t, d), lambda c: (0, 0, c)),
            anyspec,
            anyspec,
            full((8, ff)),
        ],
        out_shape=[
            jax.ShapeDtypeStruct((n, t, d), F32),
            jax.ShapeDtypeStruct((n, t, ff), BF),
            jax.ShapeDtypeStruct((n, t, ff), BF),
            half,
            half,
            jax.ShapeDtypeStruct((8, ff), F32),
        ],
        scratch_shapes=[
            pltpu.VMEM((d, d), BF),
            pltpu.VMEM((d, ff), BF),
            pltpu.VMEM((ff, d), BF),
            pltpu.VMEM((t, d), F32),
            pltpu.VMEM((n, t, d), BF),
            pltpu.VMEM((n, d, t), BF),
            pltpu.VMEM((n, t, d), BF),
            pltpu.VMEM((n, d, t), BF),
            pltpu.VMEM((nc, d, d), BF),
            pltpu.VMEM((ff, d), BF),
            pltpu.SemaphoreType.DMA((2 + ff // d, n_g)),
            pltpu.SemaphoreType.DMA((n_g * (nc + 1),)),
        ],
        name="mlp",
        compiler_params=pltpu.CompilerParams(vmem_limit_bytes=60 * 2**20),
    )(g, counts, images, o, cot, vec, bf1, *rest)


def mid_kernel(n_g, s_len, *refs):
    g_ref, cnt_ref, h_ref, cot_ref, z_ref, gu_ref, ot_ref, vec_ref = refs[:8]
    refs = refs[8:]
    rest = refs[:n_g]
    y_o, gh_o, go_o, gwo_o, gv_o = refs[n_g : n_g + 5]
    wo_s, w1_s, w2_s, xs, sem = refs[n_g + 5 :]
    i = pl.program_id(0)
    d = h_ref.shape[-1]
    ff = w1_s.shape[1]
    g = g_ref[0]

    @pl.when(i == 0)
    def _():
        co, c1, c2 = load_rest(rest, wo_s, w1_s, w2_s, sem, g, d // n_g, ff // n_g)
        for cp in co + c1 + c2:
            cp.start()
        xs[...] = jnp.zeros_like(xs)
        gwo_o[...] = jnp.zeros_like(gwo_o)
        gv_o[...] = jnp.zeros_like(gv_o)
        for cp in co + c1 + c2:
            cp.wait()

    live = (i < cnt_ref[0]).astype(F32)
    h = h_ref[0]
    y = (h + nn(z_ref[0], w2_s[...]) + vec_ref[7:8, :]) * live
    y_o[0] = y[0:s_len, :].astype(BF)
    ga2 = nt(gu_ref[0], w1_s[...])
    xhat, rstd = norm_stats(h)
    xs[0:s_len, :] = cot_ref[0].astype(F32) * live
    gh = xs[...] + norm_back(ga2, xhat, rstd, vec_ref[5:6, :])
    gh_o[0] = gh
    ghb = gh.astype(BF)
    gv_o[0:1, :] += jnp.sum(gh, 0, keepdims=True)
    gv_o[1:2, :] += jnp.sum(ga2 * xhat, 0, keepdims=True)
    gv_o[2:3, :] += jnp.sum(ga2, 0, keepdims=True)
    gwo_o[...] += nn(ot_ref[0], ghb)
    go_o[0] = nt(ghb, wo_s[...]).astype(BF)


def mid(g, counts, h, cot, z, gu, ot, vec, rest, n_g):
    n, s_len, d = cot.shape
    t = h.shape[1]
    ff = z.shape[2]
    full = lambda shape: pl.BlockSpec(shape, lambda c: (0,) * len(shape))
    per = lambda shape: pl.BlockSpec((1,) + shape, lambda i: (i, 0, 0))
    anyspec = pl.BlockSpec(memory_space=pl.ANY)
    smem = pl.BlockSpec(memory_space=pltpu.SMEM)
    return pl.pallas_call(
        functools.partial(mid_kernel, n_g, s_len),
        grid=(n,),
        in_specs=[smem, smem, per((t, d)), per((s_len, d)), per((t, ff)), per((t, ff)), per((d, t)), full(vec.shape)]
        + [anyspec] * n_g,
        out_specs=[per((s_len, d)), per((t, d)), per((t, d)), full((d, d)), full((8, d))],
        out_shape=[
            jax.ShapeDtypeStruct((n, s_len, d), BF),
            jax.ShapeDtypeStruct((n, t, d), F32),
            jax.ShapeDtypeStruct((n, t, d), BF),
            jax.ShapeDtypeStruct((d, d), F32),
            jax.ShapeDtypeStruct((8, d), F32),
        ],
        scratch_shapes=[
            pltpu.VMEM((d, d), BF),
            pltpu.VMEM((d, ff), BF),
            pltpu.VMEM((ff, d), BF),
            pltpu.VMEM((t, d), F32),
            pltpu.SemaphoreType.DMA((2 + ff // d, n_g)),
        ],
        name="mid",
        compiler_params=pltpu.CompilerParams(vmem_limit_bytes=60 * 2**20),
    )(g, counts, h, cot, z, gu, ot, vec, *rest)


def attn_bwd_kernel(n_g, s_len, *refs):
    g_ref, x_ref, q_ref, k_ref, v_ref, o_ref, kt_ref, at_ref, p_ref, go_ref, gh_ref, vec_ref, gwo_ref, gvm_ref, gb_ref = refs[:15]
    pieces = refs[15 : 15 + n_g]
    gx_o, keep_o, send_o = refs[15 + n_g : 18 + n_g]
    w_s, xs, gw_s, acc_s, stage, sem, osem = refs[18 + n_g :]
    i = pl.program_id(0)
    n = pl.num_programs(0)
    t, d = xs.shape
    rows = d // n_g
    g = g_ref[0]

    @pl.when(i == 0)
    def _():
        cps = load_rows(pieces, w_s, sem, g, rows)
        for cp in cps:
            cp.start()
        xs[...] = jnp.zeros_like(xs)
        gw_s[...] = jnp.zeros_like(gw_s)
        acc_s[...] = jnp.zeros_like(acc_s)
        for cp in cps:
            cp.wait()

    go = go_ref[0]
    prod_t = (go.astype(F32) * o_ref[0].astype(F32)).T
    lane = lax.broadcasted_iota(jnp.int32, (t, 2 * HEAD_DIM), 1)
    gqs, gks, gvs = [], [], []
    for p in range(d // (2 * HEAD_DIM)):
        c = 2 * HEAD_DIM * p
        sl = slice(c, c + 2 * HEAD_DIM)
        qp, vp, gop = q_ref[0, :, sl], v_ref[0, :, sl], go[:, sl]
        gk = jnp.zeros((t, 2 * HEAD_DIM), F32)
        gv = jnp.zeros((t, 2 * HEAD_DIM), F32)
        gqt = []
        for h in range(2):
            keep = (lane < HEAD_DIM) if h == 0 else (lane >= HEAD_DIM)
            zero = jnp.zeros_like(qp)
            r0 = c + h * HEAD_DIM
            delta = jnp.sum(prod_t[r0 : r0 + HEAD_DIM, :], 0, keepdims=True)
            pt = p_ref[0, 2 * p + h]
            dpt = nt(jnp.where(keep, vp, zero), gop)
            dst = (pt.astype(F32) * (dpt - delta)).astype(BF)
            gk = gk + nn(dst, jnp.where(keep, qp, zero))
            gv = gv + nn(pt, jnp.where(keep, gop, zero))
            gqt.append(nn(kt_ref[0, r0 : r0 + HEAD_DIM, :], dst))
        gqs.append(jnp.concatenate(gqt, 0).T * (HEAD_DIM**-0.5))
        gks.append(gk)
        gvs.append(gv)
    gqkv = jnp.concatenate(gqs + gks + gvs, 1)
    acc_s[2:3, :] += jnp.sum(gqkv[:, :d], 0, keepdims=True)
    acc_s[3:4, :] += jnp.sum(gqkv[:, 2 * d :], 0, keepdims=True)
    gb16 = gqkv.astype(BF)
    gw_s[...] += nn(at_ref[0], gb16)
    ga1 = nt(gb16, w_s[...])
    xs[0:s_len, :] = x_ref[0].astype(F32)
    xhat, rstd = norm_stats(xs[...])
    acc_s[0:1, :] += jnp.sum(ga1 * xhat, 0, keepdims=True)
    acc_s[1:2, :] += jnp.sum(ga1, 0, keepdims=True)
    gx = gh_ref[0] + norm_back(ga1, xhat, rstd, vec_ref[0:1, :])
    gx_o[0] = gx[0:s_len, :]

    @pl.when(i == n - 1)
    def _():
        low = g & 1
        ff = gb_ref.shape[1]
        frows = ff // n_g
        acc_s[4:5, :] = gvm_ref[0:1, :]
        acc_s[5:6, :] = gvm_ref[1:2, :]
        acc_s[6:7, :] = gvm_ref[2:3, :]
        acc_s[7:8, :] = gb_ref[0:1, 0:d]
        vecs = acc_s[0:8, :]
        brow = gb_ref[...]
        for s in range(n_g):
            for b in range(3):
                at = b * rows + (VROWS if b == 2 else 0)
                stage[s, at : at + rows, :] = gw_s[s * rows : (s + 1) * rows, b * d : (b + 1) * d].astype(BF)
            stage[s, 3 * rows + VROWS : 4 * rows + VROWS, :] = gwo_ref[s * rows : (s + 1) * rows, :].astype(BF)
            lo = vecs if s == 0 else pltpu.roll(vecs, d - s * rows, 1)
            hi = (brow if s == 0 else pltpu.roll(brow, ff - s * frows, 1))[:, 0:d]
            stage[s, 2 * rows : 2 * rows + VROWS, :] = jnp.concatenate([lo, hi], 0).astype(BF)
            stage[s, 4 * rows + VROWS :, :] = jnp.zeros((VROWS, d), BF)
        for parity in range(2):
            @pl.when(low == parity)
            def _():
                cps = []
                for s in range(n_g):
                    dst = keep_o if (s & 1) == parity else send_o
                    cps.append(pltpu.make_async_copy(stage.at[s], dst.at[s // 2], osem.at[s]))
                for cp in cps:
                    cp.start()
                for cp in cps:
                    cp.wait()


def attn_bwd(g, images, q, k, v, o, kt, at, pt, go, gh, vec, gwo, gvm, gb, pieces, n_g):
    n, s_len, d = images.shape
    t = q.shape[1]
    heads = d // HEAD_DIM
    rows = d // n_g
    full = lambda shape: pl.BlockSpec(shape, lambda c: (0,) * len(shape))
    per = lambda shape: pl.BlockSpec((1,) + shape, lambda i: (i, 0, 0))
    anyspec = pl.BlockSpec(memory_space=pl.ANY)
    smem = pl.BlockSpec(memory_space=pltpu.SMEM)
    half = jax.ShapeDtypeStruct((n_g // 2, 4 * rows + 2 * VROWS, d), BF)
    return pl.pallas_call(
        functools.partial(attn_bwd_kernel, n_g, s_len),
        grid=(n,),
        in_specs=[smem, per((s_len, d))]
        + [per((t, d))] * 4
        + [per((d, t))] * 2
        + [pl.BlockSpec((1, heads, t, t), lambda i: (i, 0, 0, 0))]
        + [per((t, d))] * 2
        + [full(vec.shape), full(gwo.shape), full(gvm.shape), full(gb.shape)]
        + [anyspec] * n_g,
        out_specs=[per((s_len, d)), anyspec, anyspec],
        out_shape=[jax.ShapeDtypeStruct((n, s_len, d), F32), half, half],
        scratch_shapes=[
            pltpu.VMEM((d, 3 * d), BF),
            pltpu.VMEM((t, d), F32),
            pltpu.VMEM((d, 3 * d), F32),
            pltpu.VMEM((8, d), F32),
            pltpu.VMEM((n_g, 4 * rows + 2 * VROWS, d), BF),
            pltpu.SemaphoreType.DMA((n_g,)),
            pltpu.SemaphoreType.DMA((n_g,)),
        ],
        name="attn_bwd",
        compiler_params=pltpu.CompilerParams(vmem_limit_bytes=60 * 2**20),
    )(g, images, q, k, v, o, kt, at, pt, go, gh, vec, gwo, gvm, gb, *pieces)


def pack_first_kernel(w_ref, b1_ref, *refs):
    out = refs[-1]
    rows, width = w_ref.shape
    out[0:rows, :] = w_ref[...]
    tail = jnp.zeros((1, width - rows), F32)
    vecs = [jnp.concatenate([r[...].astype(F32), tail], 1) for r in refs[:-1]]
    b1 = b1_ref[...].astype(F32)
    vecs.append(jnp.concatenate([b1, jnp.zeros((1, width - b1.shape[1]), F32)], 1))
    vecs.append(jnp.zeros((VROWS - len(vecs), width), F32))
    out[rows : rows + VROWS, :] = jnp.concatenate(vecs, 0).astype(BF)


def pack_first(w_qkv, b_fc1, vecs):
    rows, width = w_qkv.shape
    return pl.pallas_call(
        pack_first_kernel,
        out_shape=jax.ShapeDtypeStruct((rows + VROWS, width), BF),
        name="pack_first",
    )(w_qkv, b_fc1.reshape(1, -1), *[v.reshape(1, -1) for v in vecs])


def pack_rest_kernel(wo_ref, w1_ref, w2_ref, out):
    rows, d = wo_ref.shape
    frows = w2_ref.shape[0]
    out[0:frows, :] = w2_ref[...]
    for b in range(w1_ref.shape[1] // d):
        at = frows + b * rows
        out[at : at + rows, :] = w1_ref[:, b * d : (b + 1) * d]
    out[2 * frows :, :] = wo_ref[...]


def pack_rest(w_out, w_fc1, w_fc2):
    rows, d = w_out.shape
    return pl.pallas_call(
        pack_rest_kernel,
        out_shape=jax.ShapeDtypeStruct((2 * w_fc2.shape[0] + rows, d), BF),
        name="pack_rest",
    )(w_out, w_fc1, w_fc2)


def add_split_kernel(bit_ref, a_ref, b_ref, keep_o, send_o):
    bit = bit_ref[0]
    for i in range(keep_o.shape[0]):
        for out, k in ((send_o, 1 - bit), (keep_o, bit)):
            out[i] = (a_ref[2 * i + k].astype(F32) + b_ref[2 * i + k].astype(F32)).astype(BF)


def add_split(bit, a, b):
    n, r, d = a.shape
    half = jax.ShapeDtypeStruct((n // 2, r, d), BF)
    vmem = pl.BlockSpec(memory_space=pltpu.VMEM)
    return pl.pallas_call(
        add_split_kernel,
        in_specs=[pl.BlockSpec(memory_space=pltpu.SMEM), vmem, vmem],
        out_specs=[vmem, vmem],
        out_shape=[half, half],
        name="add_split",
    )(bit, a, b)


def add_kernel(a_ref, b_ref, o_ref):
    o_ref[...] = (a_ref[...].astype(F32) + b_ref[...].astype(F32)).astype(BF)


def add(a, b):
    return pl.pallas_call(add_kernel, out_shape=jax.ShapeDtypeStruct(a.shape, BF), name="add")(a, b)


def finish_mlp_kernel(bit_ref, mine, other, w2_o, w1_o):
    bit = bit_ref[0]
    rows = w1_o.shape[0]
    d = mine.shape[-1]

    def store_w2(ref):
        w2_o[...] = ref[0].astype(F32)

    def store_w1(ref):
        for b in range(w1_o.shape[1] // d):
            w1_o[:, b * d : (b + 1) * d] = ref[0, b * rows : (b + 1) * rows, :].astype(F32)

    for value in range(2):
        @pl.when(bit == value)
        def _():
            store_w2(mine if value == 0 else other)
            store_w1(other if value == 0 else mine)


def finish_mlp(bit, mine, other, rows, frows, ff):
    d = mine.shape[-1]
    vmem = pl.BlockSpec(memory_space=pltpu.VMEM)
    return pl.pallas_call(
        finish_mlp_kernel,
        in_specs=[pl.BlockSpec(memory_space=pltpu.SMEM), vmem, vmem],
        out_specs=[vmem, vmem],
        out_shape=[jax.ShapeDtypeStruct((frows, d), F32), jax.ShapeDtypeStruct((rows, ff), F32)],
        name="finish_mlp",
    )(bit, mine, other)


def finish_attn_kernel(bit_ref, mine, other, wq_o, wo_o, b1_o, *vec_o):
    bit = bit_ref[0]
    rows = wo_o.shape[0]
    d = mine.shape[-1]

    def low_half(ref):
        for b in range(2):
            wq_o[:, b * d : (b + 1) * d] = ref[0, b * rows : (b + 1) * rows, :].astype(F32)
        v = ref[0, 2 * rows : 2 * rows + VROWS, :].astype(F32)
        for j, o in enumerate(vec_o):
            o[...] = v[j : j + 1, 0:rows]
        b1_o[...] = v[9:10, 0 : b1_o.shape[1]]

    def high_half(ref):
        wq_o[:, 2 * d : 3 * d] = ref[0, 0:rows, :].astype(F32)
        wo_o[...] = ref[0, rows : 2 * rows, :].astype(F32)

    for value in range(2):
        @pl.when(bit == value)
        def _():
            low_half(mine if value == 0 else other)
            high_half(other if value == 0 else mine)


def finish_attn(bit, mine, other, rows, frows):
    d = mine.shape[-1]
    vmem = pl.BlockSpec(memory_space=pltpu.VMEM)
    shapes = [(rows, 3 * d), (rows, d), (1, frows)] + [(1, rows)] * 8
    return pl.pallas_call(
        finish_attn_kernel,
        in_specs=[pl.BlockSpec(memory_space=pltpu.SMEM), vmem, vmem],
        out_specs=[vmem] * len(shapes),
        out_shape=[jax.ShapeDtypeStruct(s, F32) for s in shapes],
        name="finish_attn",
    )(bit, mine, other)


def powers(n):
    bits = []
    while (1 << len(bits)) < n:
        bits.append(1 << len(bits))
    if (1 << len(bits)) != n:
        raise ValueError("axis size")
    return bits


def swap(a, axis, n, bit):
    return lax.ppermute(a, axis, [(i, i ^ bit) for i in range(n)])


def gather(own, n_g):
    held = {0: own}
    bits = powers(n_g)
    for bit in bits[1:] + bits[:1]:
        for m in list(held):
            held[m | bit] = swap(held[m], "grp", n_g, bit)
    return [held[m] for m in range(n_g)]


def bit_of(index, bit):
    return ((index // bit) % 2).astype(jnp.int32).reshape(1)


def reduce_shard(keep, send, n_g, n_r, g, r):
    recv = swap(send, "grp", n_g, 1)
    for bit in powers(n_g)[1:]:
        keep, send = add_split(bit_of(g, bit), keep, recv)
        recv = swap(send, "grp", n_g, bit)
    _, rows, d = keep.shape
    view = lambda a: a.reshape(2, rows // 2, d)
    keep, send = add_split(bit_of(r, 1), view(keep), view(recv))
    recv = swap(send, "rep", n_r, 1)
    mine = add(keep, recv)
    for bit in powers(n_r)[1:]:
        mine = add(mine, swap(mine, "rep", n_r, bit))
    return mine, swap(mine, "rep", n_r, 1)


def make_body(n_g, n_r):
    def body(images, cotangent, counts, ln1_gain, ln1_bias, w_qkv, b_query, b_value, w_out, b_out, ln2_gain, ln2_bias, w_fc1, b_fc1, w_fc2, b_fc2):
        g = lax.axis_index("grp")
        r = lax.axis_index("rep")
        gi = g.astype(jnp.int32).reshape(1)
        rows = w_out.shape[0]
        frows = w_fc2.shape[0]
        ff = w_fc1.shape[1]
        first = pack_first(w_qkv, b_fc1, [ln1_gain, ln1_bias, b_query, b_value, b_out, ln2_gain, ln2_bias, b_fc2])
        first = gather(first, n_g)
        rest = gather(pack_rest(w_out, w_fc1, w_fc2), n_g)
        q, k, v, o, kt, ot, at, pt, vec, bf1 = attn_fwd(gi, images, first, n_g, ff)
        h, z, gu, keep1, send1, gb = mlp(gi, counts, images, o, cotangent, vec, bf1, rest, n_g)
        y, gh, go, gwo, gvm = mid(gi, counts, h, cotangent, z, gu, ot, vec, rest, n_g)
        gx, keep2, send2 = attn_bwd(gi, images, q, k, v, o, kt, at, pt, go, gh, vec, gwo, gvm, gb, first, n_g)
        xbit = bit_of(r, 1)
        g_fc2, g_fc1 = finish_mlp(xbit, *reduce_shard(keep1, send1, n_g, n_r, g, r), rows, frows, ff)
        g_qkv, g_out, g_b1, *gv = finish_attn(xbit, *reduce_shard(keep2, send2, n_g, n_r, g, r), rows, frows)
        gv = [a.reshape(rows) for a in gv]
        return (y, gx, gv[0], gv[1], g_qkv, gv[2], gv[3], g_out, gv[4], gv[5], gv[6], g_fc1, g_b1.reshape(frows), g_fc2, gv[7])

    return body


def solution(mesh):
    rows = P(("rep", "grp"), None, None)
    vec = P("grp")
    mat = P("grp", None)
    params = (vec, vec, mat, vec, vec, mat, vec, vec, vec, mat, vec, mat, vec)
    return jax.shard_map(
        make_body(mesh.shape["grp"], mesh.shape["rep"]),
        mesh=mesh,
        in_specs=(rows, rows, P(("rep", "grp"))) + params,
        out_specs=(rows, rows) + params,
        check_vma=False,
    )
```

```python
import functools
import jax
import jax.numpy as jnp
from jax import lax
from jax.experimental import pallas as pl
from jax.experimental.pallas import tpu as pltpu
from jax.sharding import PartitionSpec as P


HEAD_DIM = 64
EPS = 1e-06
INV_ROOT2 = 0.7071067811865476
INV_ROOT2PI = 0.3989422804014327
F32 = jnp.float32
BF = jnp.bfloat16
VROWS = 16


def nn(a, b):
    return lax.dot_general(a, b, (((1,), (0,)), ((), ())), preferred_element_type=F32)


def nt(a, b):
    return lax.dot_general(a, b, (((1,), (1,)), ((), ())), preferred_element_type=F32)


def norm_stats(r):
    mean = jnp.mean(r, -1, keepdims=True)
    c = r - mean
    rstd = lax.rsqrt(jnp.mean(c * c, -1, keepdims=True) + EPS)
    return c * rstd, rstd


def norm_back(g_out, xhat, rstd, gain):
    g = g_out * gain
    return rstd * (g - jnp.mean(g, -1, keepdims=True) - xhat * jnp.mean(g * xhat, -1, keepdims=True))


def erf_poly(x_abs, e):
    t = 1.0 / (1.0 + 0.3275911 * x_abs)
    return t * (0.254829592 + t * (-0.284496736 + t * (1.421413741 + t * (-1.453152027 + t * 1.061405429)))) * e


def gelu_both(u):
    e = jnp.exp(-0.5 * u * u)
    half_tail = 0.5 * erf_poly(jnp.abs(u) * INV_ROOT2, e)
    cdf = jnp.where(u > 0, 1.0 - half_tail, half_tail)
    return u * cdf, cdf + u * e * INV_ROOT2PI


def load_rows(pieces, dst, sem, g, rows, start=0, col=None):
    copies = []
    for m, p in enumerate(pieces):
        off = pl.multiple_of((g ^ m) * rows, rows & -rows)
        to = dst.at[pl.ds(off, rows), :] if col is None else dst.at[pl.ds(off, rows), pl.ds(col, p.shape[-1])]
        copies.append(pltpu.make_async_copy(p.at[pl.ds(start, rows), :], to, sem.at[m]))
    return copies


def load_rest(pieces, wo_s, w1_s, w2_s, sem, g, rows, frows):
    d = wo_s.shape[1]
    c2 = load_rows(pieces, w2_s, sem.at[0], g, frows)
    c1 = []
    for b in range(w1_s.shape[1] // d):
        c1 += load_rows(pieces, w1_s, sem.at[2 + b], g, rows, frows + b * rows, b * d)
    co = load_rows(pieces, wo_s, sem.at[1], g, rows, 2 * frows)
    return co, c1, c2


def attn_fwd_kernel(n_g, s_len, *refs):
    g_ref, x_ref = refs[:2]
    pieces = refs[2 : 2 + n_g]
    (q_o, k_o, v_o, o_o, kt_o, ot_o, at_o, p_o, vec_o, bf1_o) = refs[2 + n_g : 12 + n_g]
    w_s, xs, vp_s, sem, vsem = refs[12 + n_g :]
    i = pl.program_id(0)
    d = x_ref.shape[-1]
    rows = d // n_g
    t = xs.shape[0]
    g = g_ref[0]

    @pl.when(i == 0)
    def _():
        cps = load_rows(pieces, w_s, sem, g, rows)
        vps = [
            pltpu.make_async_copy(p.at[pl.ds(rows, VROWS), :], vp_s.at[m], vsem.at[m])
            for m, p in enumerate(pieces)
        ]
        for c in cps + vps:
            c.start()
        xs[...] = jnp.zeros_like(xs)
        for c in cps + vps:
            c.wait()
        acc = jnp.zeros((VROWS, d), F32)
        ff = bf1_o.shape[1]
        accf = jnp.zeros((8, ff), F32)
        for m in range(n_g):
            v = vp_s[m].astype(F32)
            acc = acc + pltpu.roll(v[:, :d], (g ^ m) * rows, 1)
            b = v[8:16, :]
            b = jnp.concatenate([b, jnp.zeros((8, ff - b.shape[1]), F32)], 1)
            accf = accf + pltpu.roll(b, (g ^ m) * (ff // n_g), 1)
        vec_o[...] = acc
        bf1_o[...] = accf

    xs[0:s_len, :] = x_ref[0].astype(F32)
    xhat, _ = norm_stats(xs[...])
    a1 = xhat * vec_o[0:1, :] + vec_o[1:2, :]
    at_o[0] = xhat.T.astype(BF)
    qkv = nn(a1.astype(BF), w_s[...])
    q = ((qkv[:, :d] + vec_o[2:3, :]) * (HEAD_DIM**-0.5)).astype(BF)
    kf = qkv[:, d : 2 * d]
    k = kf.astype(BF)
    vf = qkv[:, 2 * d :] + vec_o[3:4, :]
    q_o[0] = q
    k_o[0] = k
    v_o[0] = vf.astype(BF)
    kt_o[0] = kf.T.astype(BF)
    vt = vf.T.astype(BF)
    lane = lax.broadcasted_iota(jnp.int32, (t, 2 * HEAD_DIM), 1)
    key = lax.broadcasted_iota(jnp.int32, (t, t), 0)
    for p in range(d // (2 * HEAD_DIM)):
        c = 2 * HEAD_DIM * p
        kp = k[:, c : c + 2 * HEAD_DIM]
        qp = q[:, c : c + 2 * HEAD_DIM]
        parts = []
        for h in range(2):
            keep = (lane < HEAD_DIM) if h == 0 else (lane >= HEAD_DIM)
            st = nt(jnp.where(keep, kp, jnp.zeros_like(kp)), qp)
            e = jnp.where(key < s_len, jnp.exp(st), 0.0)
            pt = (e * (1.0 / jnp.sum(e, 0, keepdims=True))).astype(BF)
            p_o[0, 2 * p + h] = pt
            r0 = c + h * HEAD_DIM
            parts.append(nn(vt[r0 : r0 + HEAD_DIM, :], pt))
        otp = jnp.concatenate(parts, 0)
        ot_o[0, c : c + 2 * HEAD_DIM, :] = otp.astype(BF)
        o_o[0, :, c : c + 2 * HEAD_DIM] = otp.T.astype(BF)


def attn_fwd(g, images, pieces, n_g, ff):
    n, s_len, d = images.shape
    t = -(-s_len // 16) * 16
    heads = d // HEAD_DIM
    nat = jax.ShapeDtypeStruct((n, t, d), BF)
    tra = jax.ShapeDtypeStruct((n, d, t), BF)
    img = pl.BlockSpec((1, t, d), lambda i: (i, 0, 0))
    imt = pl.BlockSpec((1, d, t), lambda i: (i, 0, 0))
    return pl.pallas_call(
        functools.partial(attn_fwd_kernel, n_g, s_len),
        grid=(n,),
        in_specs=[
            pl.BlockSpec(memory_space=pltpu.SMEM),
            pl.BlockSpec((1, s_len, d), lambda i: (i, 0, 0)),
        ]
        + [pl.BlockSpec(memory_space=pl.ANY)] * n_g,
        out_specs=[img, img, img, img, imt, imt, imt]
        + [
            pl.BlockSpec((1, heads, t, t), lambda i: (i, 0, 0, 0)),
            pl.BlockSpec((VROWS, d), lambda i: (0, 0)),
            pl.BlockSpec((8, ff), lambda i: (0, 0)),
        ],
        out_shape=[nat, nat, nat, nat, tra, tra, tra]
        + [
            jax.ShapeDtypeStruct((n, heads, t, t), BF),
            jax.ShapeDtypeStruct((VROWS, d), F32),
            jax.ShapeDtypeStruct((8, ff), F32),
        ],
        scratch_shapes=[
            pltpu.VMEM((d, 3 * d), BF),
            pltpu.VMEM((t, d), F32),
            pltpu.VMEM((n_g, VROWS, 3 * d), BF),
            pltpu.SemaphoreType.DMA((n_g,)),
            pltpu.SemaphoreType.DMA((n_g,)),
        ],
        name="attn_fwd",
        compiler_params=pltpu.CompilerParams(vmem_limit_bytes=60 * 2**20),
    )(g, images, *pieces)


def mlp_kernel(n_g, s_len, *refs):
    g_ref, cnt_ref, x_ref, o_ref, cot_ref, vec_ref, bf1_ref = refs[:7]
    refs = refs[7:]
    rest = refs[:n_g]
    h_o, z_o, gu_o, keep_o, send_o, gb_o = refs[n_g : n_g + 6]
    wo_s, w1_s, w2_s, xs, gy_s, gyt_s, a2_s, a2t_s, g1_s, g2_s, sem, osem = refs[n_g + 6 :]
    c = pl.program_id(0)
    n, _, d = x_ref.shape
    ff = w1_s.shape[1]
    nc = ff // d
    rows = d // n_g
    frows = ff // n_g
    g = g_ref[0]

    @pl.when(c == 0)
    def _():
        co, c1, c2 = load_rest(rest, wo_s, w1_s, w2_s, sem, g, rows, frows)
        for cp in co + c1 + c2:
            cp.start()
        xs[...] = jnp.zeros_like(xs)
        gb_o[...] = jnp.zeros_like(gb_o)
        for i in range(n):
            live = (i < cnt_ref[0]).astype(F32)
            xs[0:s_len, :] = cot_ref[i].astype(F32) * live
            gy = xs[...]
            gy_s[i] = gy.astype(BF)
            gyt_s[i] = gy.T.astype(BF)
            gb_o[0:1, 0:d] += jnp.sum(gy, 0, keepdims=True)
        for cp in co:
            cp.wait()
        for i in range(n):
            xs[0:s_len, :] = x_ref[i].astype(F32)
            h = xs[...] + nn(o_ref[i], wo_s[...]) + vec_ref[4:5, :]
            h_o[i] = h
            xhat, _ = norm_stats(h)
            a2 = xhat * vec_ref[5:6, :] + vec_ref[6:7, :]
            a2_s[i] = a2.astype(BF)
            a2t_s[i] = a2.T.astype(BF)
        for cp in c1 + c2:
            cp.wait()

    off = pl.multiple_of(c * d, 128)
    w1c = w1_s[:, pl.ds(off, d)]
    w2c = w2_s[pl.ds(off, d), :]
    b1c = bf1_ref[0:1, pl.ds(off, d)]
    g1 = jnp.zeros((d, d), F32)
    g2 = jnp.zeros((d, d), F32)
    gb = jnp.zeros((1, d), F32)
    for i in range(n):
        u = nn(a2_s[i], w1c) + b1c
        gz = nt(gy_s[i], w2c)
        z, slope = gelu_both(u)
        gu = gz * slope
        gb = gb + jnp.sum(gu, 0, keepdims=True)
        zb = z.astype(BF)
        gub = gu.astype(BF)
        z_o[i] = zb
        gu_o[i] = gub
        g2 = g2 + nn(gyt_s[i], zb)
        g1 = g1 + nn(a2t_s[i], gub)
    gb_o[1:2, pl.ds(off, d)] = gb
    g1_s[c] = g1.astype(BF)
    g2_s[pl.ds(off, d), :] = g2.T.astype(BF)

    @pl.when(c == nc - 1)
    def _():
        low = g & 1
        for parity in range(2):
            @pl.when(low == parity)
            def _():
                cps = []
                for s in range(n_g):
                    dst = keep_o if (s & 1) == parity else send_o
                    j = s // 2
                    k = len(cps)
                    cps.append(pltpu.make_async_copy(g2_s.at[pl.ds(s * frows, frows), :], dst.at[j, pl.ds(0, frows), :], osem.at[k]))
                    for b in range(nc):
                        k = len(cps)
                        cps.append(pltpu.make_async_copy(g1_s.at[b, pl.ds(s * rows, rows), :], dst.at[j, pl.ds(frows + b * rows, rows), :], osem.at[k]))
                for cp in cps:
                    cp.start()
                for cp in cps:
                    cp.wait()


def mlp(g, counts, images, o, cot, vec, bf1, rest, n_g):
    n, s_len, d = images.shape
    t = o.shape[1]
    ff = bf1.shape[1]
    nc = ff // d
    srows = ff // n_g + nc * (d // n_g)
    full = lambda shape: pl.BlockSpec(shape, lambda c: (0,) * len(shape))
    anyspec = pl.BlockSpec(memory_space=pl.ANY)
    smem = pl.BlockSpec(memory_space=pltpu.SMEM)
    half = jax.ShapeDtypeStruct((n_g // 2, srows, d), BF)
    return pl.pallas_call(
        functools.partial(mlp_kernel, n_g, s_len),
        grid=(nc,),
        in_specs=[smem, smem, full(images.shape), full(o.shape), full(cot.shape), full(vec.shape), full(bf1.shape)]
        + [anyspec] * n_g,
        out_specs=[
            full((n, t, d)),
            pl.BlockSpec((n, t, d), lambda c: (0, 0, c)),
            pl.BlockSpec((n, t, d), lambda c: (0, 0, c)),
            anyspec,
            anyspec,
            full((8, ff)),
        ],
        out_shape=[
            jax.ShapeDtypeStruct((n, t, d), F32),
            jax.ShapeDtypeStruct((n, t, ff), BF),
            jax.ShapeDtypeStruct((n, t, ff), BF),
            half,
            half,
            jax.ShapeDtypeStruct((8, ff), F32),
        ],
        scratch_shapes=[
            pltpu.VMEM((d, d), BF),
            pltpu.VMEM((d, ff), BF),
            pltpu.VMEM((ff, d), BF),
            pltpu.VMEM((t, d), F32),
            pltpu.VMEM((n, t, d), BF),
            pltpu.VMEM((n, d, t), BF),
            pltpu.VMEM((n, t, d), BF),
            pltpu.VMEM((n, d, t), BF),
            pltpu.VMEM((nc, d, d), BF),
            pltpu.VMEM((ff, d), BF),
            pltpu.SemaphoreType.DMA((2 + ff // d, n_g)),
            pltpu.SemaphoreType.DMA((n_g * (nc + 1),)),
        ],
        name="mlp",
        compiler_params=pltpu.CompilerParams(vmem_limit_bytes=60 * 2**20),
    )(g, counts, images, o, cot, vec, bf1, *rest)


def mid_kernel(n_g, s_len, *refs):
    g_ref, cnt_ref, h_ref, cot_ref, z_ref, gu_ref, ot_ref, vec_ref = refs[:8]
    refs = refs[8:]
    rest = refs[:n_g]
    y_o, gh_o, go_o, gwo_o, gv_o = refs[n_g : n_g + 5]
    wo_s, w1_s, w2_s, xs, sem = refs[n_g + 5 :]
    i = pl.program_id(0)
    d = h_ref.shape[-1]
    ff = w1_s.shape[1]
    g = g_ref[0]

    @pl.when(i == 0)
    def _():
        co, c1, c2 = load_rest(rest, wo_s, w1_s, w2_s, sem, g, d // n_g, ff // n_g)
        for cp in co + c1 + c2:
            cp.start()
        xs[...] = jnp.zeros_like(xs)
        gwo_o[...] = jnp.zeros_like(gwo_o)
        gv_o[...] = jnp.zeros_like(gv_o)
        for cp in co + c1 + c2:
            cp.wait()

    live = (i < cnt_ref[0]).astype(F32)
    h = h_ref[0]
    y = (h + nn(z_ref[0], w2_s[...]) + vec_ref[7:8, :]) * live
    y_o[0] = y[0:s_len, :].astype(BF)
    ga2 = nt(gu_ref[0], w1_s[...])
    xhat, rstd = norm_stats(h)
    xs[0:s_len, :] = cot_ref[0].astype(F32) * live
    gh = xs[...] + norm_back(ga2, xhat, rstd, vec_ref[5:6, :])
    gh_o[0] = gh
    ghb = gh.astype(BF)
    gv_o[0:1, :] += jnp.sum(gh, 0, keepdims=True)
    gv_o[1:2, :] += jnp.sum(ga2 * xhat, 0, keepdims=True)
    gv_o[2:3, :] += jnp.sum(ga2, 0, keepdims=True)
    gwo_o[...] += nn(ot_ref[0], ghb)
    go_o[0] = nt(ghb, wo_s[...]).astype(BF)


def mid(g, counts, h, cot, z, gu, ot, vec, rest, n_g):
    n, s_len, d = cot.shape
    t = h.shape[1]
    ff = z.shape[2]
    full = lambda shape: pl.BlockSpec(shape, lambda c: (0,) * len(shape))
    per = lambda shape: pl.BlockSpec((1,) + shape, lambda i: (i, 0, 0))
    anyspec = pl.BlockSpec(memory_space=pl.ANY)
    smem = pl.BlockSpec(memory_space=pltpu.SMEM)
    return pl.pallas_call(
        functools.partial(mid_kernel, n_g, s_len),
        grid=(n,),
        in_specs=[smem, smem, per((t, d)), per((s_len, d)), per((t, ff)), per((t, ff)), per((d, t)), full(vec.shape)]
        + [anyspec] * n_g,
        out_specs=[per((s_len, d)), per((t, d)), per((t, d)), full((d, d)), full((8, d))],
        out_shape=[
            jax.ShapeDtypeStruct((n, s_len, d), BF),
            jax.ShapeDtypeStruct((n, t, d), F32),
            jax.ShapeDtypeStruct((n, t, d), BF),
            jax.ShapeDtypeStruct((d, d), F32),
            jax.ShapeDtypeStruct((8, d), F32),
        ],
        scratch_shapes=[
            pltpu.VMEM((d, d), BF),
            pltpu.VMEM((d, ff), BF),
            pltpu.VMEM((ff, d), BF),
            pltpu.VMEM((t, d), F32),
            pltpu.SemaphoreType.DMA((2 + ff // d, n_g)),
        ],
        name="mid",
        compiler_params=pltpu.CompilerParams(vmem_limit_bytes=60 * 2**20),
    )(g, counts, h, cot, z, gu, ot, vec, *rest)


def attn_bwd_kernel(n_g, first, last, *refs):
    refs = list(refs)
    q_ref, _, v_ref, o_ref, kt_ref, xt_ref, p_ref, go_ref = refs[:8]
    refs = refs[8:]
    if not first:
        x_in, acc_in = refs[:2]
        refs = refs[2:]
    if last:
        g_ref, vec_ref, gwo_ref, gvm_ref, gb_ref = refs[:5]
        pieces = refs[5 : 5 + n_g]
        refs = refs[5 + n_g :]
        gq_o, keep_o, send_o, x_s, acc_s, w_s, stage, sem, osem = refs
    else:
        gq_o, x_s, acc_s = refs
    i = pl.program_id(0)
    n = pl.num_programs(0)
    t, d = q_ref.shape[1:]
    rows = d // n_g

    @pl.when(i == 0)
    def _():
        if last:
            for cp in load_rows(pieces, w_s, sem, g_ref[0], rows):
                cp.start()
        if first:
            x_s[...] = jnp.zeros_like(x_s)
            acc_s[...] = jnp.zeros_like(acc_s)
        else:
            x_s[...] = x_in[...]
            acc_s[...] = acc_in[...]

    go = go_ref[0]
    prod_t = (go.astype(F32) * o_ref[0].astype(F32)).T
    lane = lax.broadcasted_iota(jnp.int32, (t, 2 * HEAD_DIM), 1)
    gqs, gks, gvs = [], [], []
    for p in range(d // (2 * HEAD_DIM)):
        c = 2 * HEAD_DIM * p
        sl = slice(c, c + 2 * HEAD_DIM)
        qp, vp, gop = q_ref[0, :, sl], v_ref[0, :, sl], go[:, sl]
        gk = jnp.zeros((t, 2 * HEAD_DIM), F32)
        gv = jnp.zeros((t, 2 * HEAD_DIM), F32)
        gqt = []
        for h in range(2):
            keep = (lane < HEAD_DIM) if h == 0 else (lane >= HEAD_DIM)
            zero = jnp.zeros_like(qp)
            r0 = c + h * HEAD_DIM
            delta = jnp.sum(prod_t[r0 : r0 + HEAD_DIM, :], 0, keepdims=True)
            pt = p_ref[0, 2 * p + h]
            dpt = nt(jnp.where(keep, vp, zero), gop)
            dst = (pt.astype(F32) * (dpt - delta)).astype(BF)
            gk = gk + nn(dst, jnp.where(keep, qp, zero))
            gv = gv + nn(pt, jnp.where(keep, gop, zero))
            gqt.append(nn(kt_ref[0, r0 : r0 + HEAD_DIM, :], dst))
        gqs.append(jnp.concatenate(gqt, 0).T * (HEAD_DIM**-0.5))
        gks.append(gk)
        gvs.append(gv)
    gqkv = jnp.concatenate(gqs + gks + gvs, 1)
    acc_s[0:1, :] += jnp.sum(gqkv, 0, keepdims=True)
    gb16 = gqkv.astype(BF)
    gq_o[0] = gb16
    x_s[...] += nn(xt_ref[0], gb16)
    if not last:
        return

    @pl.when(i == n - 1)
    def _():
        for cp in load_rows(pieces, w_s, sem, g_ref[0], rows):
            cp.wait()
        low = g_ref[0] & 1
        ff = gb_ref.shape[1]
        frows = ff // n_g
        x = x_s[...]
        w = w_s[...]
        col = acc_s[0:1, :]
        g_gain = jnp.broadcast_to(jnp.sum(w.astype(F32) * x, 1, keepdims=True), (d, 128)).T[0:1, :]
        hi = col.astype(BF)
        lo = (col - hi.astype(F32)).astype(BF)
        pad = jnp.zeros((14, 3 * d), BF)
        g_bias = jnp.sum(nt(jnp.concatenate([hi, lo, pad], 0), w), 0, keepdims=True)
        vecs = jnp.concatenate(
            [g_gain, g_bias, col[:, 0:d], col[:, 2 * d : 3 * d], gvm_ref[0:3, :], gb_ref[0:1, 0:d]], 0
        )
        gain = jnp.broadcast_to(vec_ref[0:1, :], (128, d)).T[:, 0:1]
        bias = jnp.broadcast_to(vec_ref[1:2, :], (128, d)).T[:, 0:1]
        gw = (gain * x + bias * col).astype(BF)
        brow = gb_ref[...]
        for s in range(n_g):
            for b in range(3):
                at = b * rows + (VROWS if b == 2 else 0)
                stage[s, at : at + rows, :] = gw[s * rows : (s + 1) * rows, b * d : (b + 1) * d]
            stage[s, 3 * rows + VROWS : 4 * rows + VROWS, :] = gwo_ref[s * rows : (s + 1) * rows, :].astype(BF)
            lov = vecs if s == 0 else pltpu.roll(vecs, d - s * rows, 1)
            hiv = (brow if s == 0 else pltpu.roll(brow, ff - s * frows, 1))[:, 0:d]
            stage[s, 2 * rows : 2 * rows + VROWS, :] = jnp.concatenate([lov, hiv], 0).astype(BF)
            stage[s, 4 * rows + VROWS :, :] = jnp.zeros((VROWS, d), BF)
        for parity in range(2):
            @pl.when(low == parity)
            def _():
                cps = []
                for s in range(n_g):
                    dst = keep_o if (s & 1) == parity else send_o
                    cps.append(pltpu.make_async_copy(stage.at[s], dst.at[s // 2], osem.at[s]))
                for cp in cps:
                    cp.start()
                for cp in cps:
                    cp.wait()


def attn_bwd(at, count, acts, carry, tail, n_g):
    q = acts[0]
    _, t, d = q.shape
    heads = d // HEAD_DIM
    rows = d // n_g
    full = lambda a: pl.BlockSpec(a.shape, lambda c: (0,) * a.ndim)
    per = lambda shape: pl.BlockSpec((1,) + shape, lambda i: (i + at if at else i,) + (0,) * len(shape))
    anyspec = pl.BlockSpec(memory_space=pl.ANY)
    smem = pl.BlockSpec(memory_space=pltpu.SMEM)
    sums = [jax.ShapeDtypeStruct((d, 3 * d), F32), jax.ShapeDtypeStruct((8, 3 * d), F32)]
    gq_spec = pl.BlockSpec((1, t, 3 * d), lambda i: (i, 0, 0))
    gq_shape = jax.ShapeDtypeStruct((count, t, 3 * d), BF)
    in_specs = [per((t, d))] * 4 + [per((d, t))] * 2 + [per((heads, t, t)), per((t, d))] + [full(a) for a in carry]
    operands = list(acts) + list(carry)
    if tail is None:
        out_specs, out_shape = [gq_spec] + [full(a) for a in sums], [gq_shape] + sums
        scratch = []
    else:
        half = jax.ShapeDtypeStruct((n_g // 2, 4 * rows + 2 * VROWS, d), BF)
        g, vec, gwo, gvm, gb, pieces = tail
        operands += [g, vec, gwo, gvm, gb, *pieces]
        in_specs += [smem] + [full(a) for a in (vec, gwo, gvm, gb)] + [anyspec] * n_g
        out_specs, out_shape = [gq_spec, anyspec, anyspec], [gq_shape, half, half]
        scratch = [
            pltpu.VMEM(sums[0].shape, F32),
            pltpu.VMEM(sums[1].shape, F32),
            pltpu.VMEM((d, 3 * d), BF),
            pltpu.VMEM((n_g, 4 * rows + 2 * VROWS, d), BF),
            pltpu.SemaphoreType.DMA((n_g,)),
            pltpu.SemaphoreType.DMA((n_g,)),
        ]
    return pl.pallas_call(
        functools.partial(attn_bwd_kernel, n_g, not carry, tail is not None),
        grid=(count,),
        in_specs=in_specs,
        out_specs=out_specs,
        out_shape=out_shape,
        scratch_shapes=scratch,
        name="attn_bwd",
        compiler_params=pltpu.CompilerParams(vmem_limit_bytes=60 * 2**20),
    )(*operands)


def input_grad_kernel(n_g, s_len, parts, *refs):
    g_ref, x_ref, gh_ref, vec_ref = refs[:4]
    gq_refs = refs[4 : 4 + parts]
    pieces = refs[4 + parts : 4 + parts + n_g]
    gx_o, w_s, xs, sem = refs[4 + parts + n_g :]
    i = pl.program_id(0)
    n = pl.num_programs(0)
    d = xs.shape[1]

    @pl.when(i == 0)
    def _():
        cps = load_rows(pieces, w_s, sem, g_ref[0], d // n_g)
        for cp in cps:
            cp.start()
        xs[...] = jnp.zeros_like(xs)
        for cp in cps:
            cp.wait()

    gq = gq_refs[0][0]
    for j in range(1, parts):
        gq = jnp.where(i >= j * (n // parts), gq_refs[j][0], gq)
    ga1 = nt(gq, w_s[...])
    xs[0:s_len, :] = x_ref[0].astype(F32)
    xhat, rstd = norm_stats(xs[...])
    gx = gh_ref[0] + norm_back(ga1, xhat, rstd, vec_ref[0:1, :])
    gx_o[0] = gx[0:s_len, :]


def input_grad(g, images, gh, vec, gqs, pieces, n_g):
    n, s_len, d = images.shape
    t = gh.shape[1]
    parts = len(gqs)
    each = n // parts
    per = lambda shape: pl.BlockSpec((1,) + shape, lambda i: (i, 0, 0))

    def part(j):
        return pl.BlockSpec((1, t, 3 * d), lambda i: (jnp.clip(i - j * each, 0, each - 1), 0, 0))

    return pl.pallas_call(
        functools.partial(input_grad_kernel, n_g, s_len, parts),
        grid=(n,),
        in_specs=[pl.BlockSpec(memory_space=pltpu.SMEM), per((s_len, d)), per((t, d)), pl.BlockSpec(vec.shape, lambda i: (0, 0))]
        + [part(j) for j in range(parts)]
        + [pl.BlockSpec(memory_space=pl.ANY)] * n_g,
        out_specs=per((s_len, d)),
        out_shape=jax.ShapeDtypeStruct((n, s_len, d), F32),
        scratch_shapes=[pltpu.VMEM((d, 3 * d), BF), pltpu.VMEM((t, d), F32), pltpu.SemaphoreType.DMA((n_g,))],
        name="input_grad",
        compiler_params=pltpu.CompilerParams(vmem_limit_bytes=60 * 2**20),
    )(g, images, gh, vec, *gqs, *pieces)


def pack_first_kernel(w_ref, b1_ref, *refs):
    out = refs[-1]
    rows, width = w_ref.shape
    out[0:rows, :] = w_ref[...]
    tail = jnp.zeros((1, width - rows), F32)
    vecs = [jnp.concatenate([r[...].astype(F32).reshape(1, rows), tail], 1) for r in refs[:-1]]
    b1 = b1_ref[...].astype(F32).reshape(1, -1)
    vecs.append(jnp.concatenate([b1, jnp.zeros((1, width - b1.shape[1]), F32)], 1))
    vecs.append(jnp.zeros((VROWS - len(vecs), width), F32))
    out[rows : rows + VROWS, :] = jnp.concatenate(vecs, 0).astype(BF)


def pack_first(w_qkv, b_fc1, vecs):
    rows, width = w_qkv.shape
    return pl.pallas_call(
        pack_first_kernel,
        out_shape=jax.ShapeDtypeStruct((rows + VROWS, width), BF),
        name="pack_first",
    )(w_qkv, b_fc1, *vecs)


def pack_rest_kernel(wo_ref, w1_ref, w2_ref, out):
    rows, d = wo_ref.shape
    frows = w2_ref.shape[0]
    out[0:frows, :] = w2_ref[...]
    for b in range(w1_ref.shape[1] // d):
        at = frows + b * rows
        out[at : at + rows, :] = w1_ref[:, b * d : (b + 1) * d]
    out[2 * frows :, :] = wo_ref[...]


def pack_rest(w_out, w_fc1, w_fc2):
    rows, d = w_out.shape
    return pl.pallas_call(
        pack_rest_kernel,
        out_shape=jax.ShapeDtypeStruct((2 * w_fc2.shape[0] + rows, d), BF),
        name="pack_rest",
    )(w_out, w_fc1, w_fc2)


def total(a, b):
    return (a.astype(F32) + b.astype(F32)).astype(BF)


def add_split(bit, a, b):
    n, r, d = a.shape
    pick = lambda x, k: lax.dynamic_index_in_dim(x.reshape(n // 2, 2, r, d), k, 1, keepdims=False)
    return total(pick(a, bit), pick(b, bit)), total(pick(a, 1 - bit), pick(b, 1 - bit))


def finish_mlp_kernel(bit_ref, mine, other, w2_o, w1_o):
    bit = bit_ref[0]
    rows = w1_o.shape[0]
    d = mine.shape[-1]

    def store_w2(ref):
        w2_o[...] = ref[0].astype(F32)

    def store_w1(ref):
        for b in range(w1_o.shape[1] // d):
            w1_o[:, b * d : (b + 1) * d] = ref[0, b * rows : (b + 1) * rows, :].astype(F32)

    for value in range(2):
        @pl.when(bit == value)
        def _():
            store_w2(mine if value == 0 else other)
            store_w1(other if value == 0 else mine)


def finish_mlp(bit, mine, other, rows, frows, ff):
    d = mine.shape[-1]
    vmem = pl.BlockSpec(memory_space=pltpu.VMEM)
    return pl.pallas_call(
        finish_mlp_kernel,
        in_specs=[pl.BlockSpec(memory_space=pltpu.SMEM), vmem, vmem],
        out_specs=[vmem, vmem],
        out_shape=[jax.ShapeDtypeStruct((frows, d), F32), jax.ShapeDtypeStruct((rows, ff), F32)],
        name="finish_mlp",
    )(bit, mine, other)


def finish_attn_kernel(bit_ref, mine, other, wq_o, wo_o, b1_o, *vec_o):
    bit = bit_ref[0]
    rows = wo_o.shape[0]
    d = mine.shape[-1]

    def low_half(ref):
        for b in range(2):
            wq_o[:, b * d : (b + 1) * d] = ref[0, b * rows : (b + 1) * rows, :].astype(F32)
        v = ref[0, 2 * rows : 2 * rows + VROWS, :].astype(F32)
        for j, o in enumerate(vec_o):
            o[...] = v[j, 0:rows]
        b1_o[...] = v[9, 0 : b1_o.shape[0]]

    def high_half(ref):
        wq_o[:, 2 * d : 3 * d] = ref[0, 0:rows, :].astype(F32)
        wo_o[...] = ref[0, rows : 2 * rows, :].astype(F32)

    for value in range(2):
        @pl.when(bit == value)
        def _():
            low_half(mine if value == 0 else other)
            high_half(other if value == 0 else mine)


def finish_attn(bit, mine, other, rows, frows):
    d = mine.shape[-1]
    vmem = pl.BlockSpec(memory_space=pltpu.VMEM)
    shapes = [(rows, 3 * d), (rows, d), (frows,)] + [(rows,)] * 8
    return pl.pallas_call(
        finish_attn_kernel,
        in_specs=[pl.BlockSpec(memory_space=pltpu.SMEM), vmem, vmem],
        out_specs=[vmem] * len(shapes),
        out_shape=[jax.ShapeDtypeStruct(s, F32) for s in shapes],
        name="finish_attn",
    )(bit, mine, other)


def powers(n):
    bits = []
    while (1 << len(bits)) < n:
        bits.append(1 << len(bits))
    if (1 << len(bits)) != n:
        raise ValueError("axis size")
    return bits


def swap(a, axis, n, bit):
    return lax.ppermute(a, axis, [(i, i ^ bit) for i in range(n)])


def gather_far(own, n_g):
    held = {0: own}
    for bit in powers(n_g)[1:]:
        for m in list(held):
            held[m | bit] = swap(held[m], "grp", n_g, bit)
    return held


def gather_near(held, n_g):
    held = dict(held)
    for m in list(held):
        held[m | 1] = swap(held[m], "grp", n_g, 1)
    return [held[m] for m in range(n_g)]


def bit_of(index, bit):
    return lax.shift_right_logical(index, bit.bit_length() - 1) & 1


def reduce_group(keep, send, n_g, g):
    recv = swap(send, "grp", n_g, 1)
    for bit in powers(n_g)[1:]:
        keep, send = add_split(bit_of(g, bit), keep, recv)
        recv = swap(send, "grp", n_g, bit)
    return keep, recv


def halve(keep, recv, r):
    _, rows, d = keep.shape
    view = lambda a: a.reshape(2, rows // 2, d)
    return add_split(bit_of(r, 1), view(keep), view(recv))


def reduce_replicas(keep, send, n_r):
    mine = total(keep, swap(send, "rep", n_r, 1))
    for bit in powers(n_r)[1:]:
        mine = total(mine, swap(mine, "rep", n_r, bit))
    return mine, swap(mine, "rep", n_r, 1)


def make_body(n_g, n_r):
    def body(images, cotangent, counts, ln1_gain, ln1_bias, w_qkv, b_query, b_value, w_out, b_out, ln2_gain, ln2_bias, w_fc1, b_fc1, w_fc2, b_fc2):
        g = lax.axis_index("grp").astype(jnp.int32)
        r = lax.axis_index("rep").astype(jnp.int32)
        gi = g.reshape(1)
        n = images.shape[0]
        rows = w_out.shape[0]
        frows = w_fc2.shape[0]
        ff = w_fc1.shape[1]
        first = pack_first(w_qkv, b_fc1, [ln1_gain, ln1_bias, b_query, b_value, b_out, ln2_gain, ln2_bias, b_fc2])
        first = gather_near(gather_far(first, n_g), n_g)
        rest = pack_rest(w_out, w_fc1, w_fc2)
        rest = gather_near(gather_far(rest, n_g), n_g)
        q, k, v, o, kt, ot, xt, pt, vec, bf1 = attn_fwd(gi, images, first, n_g, ff)
        h, z, gu, keep1, send1, gb = mlp(gi, counts, images, o, cotangent, vec, bf1, rest, n_g)
        keep1, recv1 = reduce_group(keep1, send1, n_g, g)
        y, gh, go, gwo, gvm = mid(gi, counts, h, cotangent, z, gu, ot, vec, rest, n_g)
        acts = (q, k, v, o, kt, xt, pt, go)
        gq_a, *carry = attn_bwd(0, n // 2, acts, (), None, n_g)
        keep1, send1 = halve(keep1, recv1, r)
        send1, carry = lax.optimization_barrier((send1, carry))
        gq_b, keep2, send2 = attn_bwd(n // 2, n - n // 2, acts, carry, (gi, vec, gwo, gvm, gb, first), n_g)
        gx = input_grad(gi, images, gh, vec, (gq_a, gq_b), first, n_g)
        xbit = bit_of(r, 1).reshape(1)
        keep2, recv2 = reduce_group(keep2, send2, n_g, g)
        g_fc2, g_fc1 = finish_mlp(xbit, *reduce_replicas(keep1, send1, n_r), rows, frows, ff)
        keep2, send2 = halve(keep2, recv2, r)
        g_qkv, g_out, g_b1, *gv = finish_attn(xbit, *reduce_replicas(keep2, send2, n_r), rows, frows)
        return (y, gx, gv[0], gv[1], g_qkv, gv[2], gv[3], g_out, gv[4], gv[5], gv[6], g_fc1, g_b1, g_fc2, gv[7])

    return body


def solution(mesh):
    rows = P(("rep", "grp"), None, None)
    vec = P("grp")
    mat = P("grp", None)
    params = (vec, vec, mat, vec, vec, mat, vec, vec, vec, mat, vec, mat, vec)
    return jax.shard_map(
        make_body(mesh.shape["grp"], mesh.shape["rep"]),
        mesh=mesh,
        in_specs=(rows, rows, P(("rep", "grp"))) + params,
        out_specs=(rows, rows) + params,
        check_vma=False,
    )
```
